256 devices in a mesh: chan: 16 (over y, x), filt: 8 (over z), space: 2 (over core).
Axes of the slice: x: 4, y: 4, z: 8, core: 2. Of those that a mesh axis runs over, the one named last changes fastest.
Arguments:
- voxels: bfloat16 [128, 512, 256], P(('space', 'filt'), 'chan'), may hold values from -6 to 6
- filters: bfloat16 [27, 512, 512], P(None, 'chan', 'filt'), may hold values from -0.0546875 to 0.0546875
- upstream: bfloat16 [128, 512, 256], P(('space', 'chan'), 'filt'), may hold values from -6 to 6
Outputs:
- responses: bfloat16 [128, 512, 256], P(('space', 'chan'), 'filt')
- voxel_grad: bfloat16 [128, 512, 256], P(('space', 'filt'), 'chan')
- filter_grad: float32 [27, 512, 512], P(None, 'chan', 'filt')
The draws below stay inside these ranges and needn't reach their ends.
All inputs are finite; a program needn't handle non-finite values.
Results may differ from the reference program's by a relative error of at most 0.001.
Values may be sent and summed in bfloat16 or wider, within the bound.
A program may use at most 64 MiB of HBM per device.

```python
import jax
import jax.numpy as jnp
from jax import lax

C = 512
F = 512
PLANE_Y = 16
PLANE_Z = 16
NX = 128
PLANE = 256


def raised(array, key, source, target, parts, factor):
    def block_of(axis_at):
        return (jnp.arange(array.shape[axis_at]) // (array.shape[axis_at] // parts)).reshape((-1,) + (1,) * (array.ndim - 1 - axis_at))

    first = jax.random.permutation(key, parts)[block_of(target)]
    other_side = (block_of(target) + parts // 2) % parts
    return jnp.where((block_of(source) == first) | (block_of(source) == other_side), factor * array, array)


def steps_of(rng, extent, shards, smallest, high):
    factor_of, own = 1.0, jax.random.fold_in(rng, 6)
    for dim, parts in shards:
        heights = jnp.exp(jax.random.uniform(jax.random.fold_in(own, dim), (parts,), jnp.float32, smallest / len(shards), high / len(shards)))
        factor_of = factor_of * jnp.repeat(heights, extent[dim] // parts).reshape([-1 if axis == dim else 1 for axis in range(len(extent))])
    return factor_of


def gaussian(stream_key, dims, spread, bound, split=(), dtype=jnp.bfloat16):
    values = jax.random.normal(stream_key, dims, jnp.float32) * spread
    if len(split) > 0:
        values = steps_of(stream_key, dims, split, -0.22, 0.18) * values
    return jnp.clip(values, min=-bound, max=bound).astype(dtype)


def bell_draw_with(key, shape, deviation, limit, pieces, heavy, held_as=jnp.bfloat16):
    values = deviation * jax.random.normal(key, shape, jnp.float32)
    if pieces:
        values = values * steps_of(key, shape, pieces, -0.22, 0.18)
    return jnp.clip(raised(values, jax.random.fold_in(key, 3), *heavy), -limit, limit).astype(held_as)


def setup_inputs(seed: int = 0) -> dict:
    key_of = jax.random.split(jax.random.key(seed), 4)
    return {
        "voxels": bell_draw_with(key_of[0], (NX, C, PLANE), 1.0, 6.0, ((0, 16), (1, 16)), (1, 0, 16, 2.0)),
        "filters": gaussian(key_of[1], (27, C, F), (27 * C) ** -0.5, 0.0546875, ((1, 16), (2, 8))),
        "upstream": bell_draw_with(key_of[2], (NX, F, PLANE), 1.0, 6.0, ((0, 32), (1, 8)), (1, 0, 32, 2.75)),
    }


def to_volume(field):
    shaped = field.reshape(field.shape[0], field.shape[1], PLANE_Y, PLANE_Z)
    return shaped.transpose(1, 0, 2, 3)[None]

def from_volume(volume):
    shaped = volume[0].transpose(1, 0, 2, 3)
    return shaped.reshape(shaped.shape[0], shaped.shape[1], PLANE_Y * PLANE_Z)

def convolve(volume, weights):
    return lax.conv_general_dilated(volume, weights, (1, 1, 1), ((1, 1), (1, 1), (1, 1)), dimension_numbers=('NCDHW', 'OIDHW', 'NCDHW'), precision=lax.Precision.HIGHEST)

def reference(voxels, filters, upstream):
    inputs = to_volume(voxels.astype(jnp.float32))
    kernel = filters.astype(jnp.float32).reshape(3, 3, 3, C, F).transpose(4, 3, 0, 1, 2)
    result, pullback = jax.vjp(convolve, inputs, kernel)
    volume_grad, kernel_grad = pullback(to_volume(upstream.astype(jnp.float32)))
    responses = from_volume(result).astype(jnp.bfloat16)
    voxel_grad = from_volume(volume_grad).astype(jnp.bfloat16)
    scaling = jnp.sqrt(jnp.float32(NX * PLANE_Y * PLANE_Z))
    filter_grad = kernel_grad.transpose(2, 3, 4, 1, 0).reshape(27, C, F) / scaling
    return (responses, voxel_grad, filter_grad)
```

```python
import jax
import jax.numpy as jnp
from jax import lax
from jax.experimental import pallas as pl
from jax.experimental.pallas import tpu as pltpu
from jax.sharding import PartitionSpec as P

OFFSETS = [(dy, dz) for dy in (-1, 0, 1) for dz in (-1, 0, 1)]
GROUP = 4


def tap_masks():
    lane = lax.broadcasted_iota(jnp.int32, (1, 256), 1)
    z = lane & 15
    y = lane >> 4
    out = []
    for dy, dz in OFFSETS:
        ok = (y + dy >= 0) & (y + dy < 16) & (z + dz >= 0) & (z + dz < 16)
        out.append(jnp.where(ok, 1.0, 0.0).astype(jnp.float32))
    return out


def columns(x, masks, sign):
    parts = []
    for i in range(9):
        dy, dz = OFFSETS[i]
        off = sign * (dy * 16 + dz)
        if off == 0:
            parts.append(x)
            continue
        mask = masks[i if sign > 0 else 8 - i]
        parts.append(pltpu.roll(x, (-off) % 256, 1) * mask.astype(x.dtype))
    return jnp.concatenate(parts, axis=0)


def spread(acc, base, width, ys):
    n = len(ys)
    for i in range(n + 2):
        total = None
        for j in range(max(0, i - 2), min(n, i + 1)):
            part = ys[j][width * (i - j) : width * (i - j + 1), :]
            total = part if total is None else total + part
        rows = pl.ds(pl.multiple_of(base + i * width, width), width)
        acc[rows, :] = acc[rows, :] + total


def conv_kernel(xv, uv, fl, pf, pd, dw, wf, wd, accf, accd, accw):
    for a in range(3):
        w = fl[9 * a : 9 * a + 9].reshape(288, 64)
        wf[64 * (2 - a) : 64 * (3 - a), :] = w.astype(jnp.float32).T.astype(jnp.bfloat16)
        for t in range(9):
            wd[32 * a : 32 * a + 32, 64 * t : 64 * t + 64] = fl[9 * a + t]
    accf[...] = jnp.zeros_like(accf)
    accd[...] = jnp.zeros_like(accd)
    accw[...] = jnp.zeros_like(accw)
    masks = tap_masks()

    def forward(b):
        cols = [columns(xv[b * GROUP + j + 1], masks, 1) for j in range(GROUP)]
        ys = [jnp.dot(wf[...], c, preferred_element_type=jnp.float32) for c in cols]
        spread(accf, (b * GROUP + 1) * 64, 64, ys)
        around = [
            uv[pl.ds(pl.multiple_of((b * GROUP + j) * 64, 64), 192), :] for j in range(GROUP)
        ]
        accw[...] = accw[...] + lax.dot_general(
            jnp.concatenate(cols, axis=1),
            jnp.concatenate(around, axis=1),
            (((1,), (1,)), ((), ())),
            preferred_element_type=jnp.float32,
        )

    def backward(b):
        ys = []
        for j in range(GROUP):
            plane = uv[pl.ds(pl.multiple_of((b * GROUP + j + 1) * 64, 64), 64), :]
            ys.append(
                jnp.dot(wd[...], columns(plane, masks, -1), preferred_element_type=jnp.float32)
            )
        spread(accd, (b * GROUP + 1) * 32, 32, ys)

    for q in (0, 65):
        spread(accf, q * 64, 64, [jnp.dot(wf[...], columns(xv[q], masks, 1), preferred_element_type=jnp.float32)])
        plane = uv[q * 64 : q * 64 + 64, :]
        spread(accd, q * 32, 32, [jnp.dot(wd[...], columns(plane, masks, -1), preferred_element_type=jnp.float32)])

    @pl.loop(0, 64 // GROUP)
    def _(b):
        forward(b)
        backward(b)

    pf[...] = accf[128 : 128 + 4096, :]
    pd[...] = accd[64 : 64 + 2048, :]
    for a in range(3):
        for t in range(9):
            dw[9 * a + t] = accw[32 * t : 32 * t + 32, 64 * (2 - a) : 64 * (3 - a)]


def convolutions(xv, uv, fl):
    return pl.pallas_call(
        conv_kernel,
        out_shape=(
            jax.ShapeDtypeStruct((4096, 256), jnp.float32),
            jax.ShapeDtypeStruct((2048, 256), jnp.float32),
            jax.ShapeDtypeStruct((27, 32, 64), jnp.float32),
        ),
        in_specs=[pl.BlockSpec(memory_space=pltpu.VMEM)] * 3,
        out_specs=[pl.BlockSpec(memory_space=pltpu.VMEM)] * 3,
        scratch_shapes=[
            pltpu.VMEM((192, 288), jnp.bfloat16),
            pltpu.VMEM((96, 576), jnp.bfloat16),
            pltpu.VMEM((68 * 64, 256), jnp.float32),
            pltpu.VMEM((68 * 32, 256), jnp.float32),
            pltpu.VMEM((288, 192), jnp.float32),
        ],
        compiler_params=pltpu.CompilerParams(vmem_limit_bytes=60 * 2**20),
    )(xv, uv, fl)


def with_halo(block):
    low = lax.ppermute(block[-1:], "space", [(0, 1)])
    high = lax.ppermute(block[:1], "space", [(1, 0)])
    return jnp.concatenate([low, block, high], axis=0)


def local(voxels, filters, upstream):
    xv = with_halo(lax.all_gather(voxels, "filt", axis=0, tiled=True))
    uv = with_halo(lax.all_gather(upstream, "chan", axis=0, tiled=True))
    pf, pd, dw = convolutions(xv, uv.reshape(66 * 64, 256), filters)
    responses = lax.psum_scatter(pf.reshape(64, 64, 256), "chan", scatter_dimension=0, tiled=True)
    voxel_grad = lax.psum_scatter(pd.reshape(64, 32, 256), "filt", scatter_dimension=0, tiled=True)
    filter_grad = lax.psum(dw, "space") / jnp.sqrt(jnp.float32(128 * 256))
    return (responses.astype(jnp.bfloat16), voxel_grad.astype(jnp.bfloat16), filter_grad)


def solution(mesh):
    return jax.shard_map(
        local,
        mesh=mesh,
        in_specs=(
            P(("space", "filt"), "chan", None),
            P(None, "chan", "filt"),
            P(("space", "chan"), "filt", None),
        ),
        out_specs=(
            P(("space", "chan"), "filt", None),
            P(("space", "filt"), "chan", None),
            P(None, "chan", "filt"),
        ),
        check_vma=False,
    )
```

```python
import jax
import jax.numpy as jnp
from jax import lax
from jax.experimental import pallas as pl
from jax.experimental.pallas import tpu as pltpu
from jax.sharding import PartitionSpec as P

OFFSETS = [(dy, dz) for dy in (-1, 0, 1) for dz in (-1, 0, 1)]
GROUP = 4
COPIES = 105


def tap_masks():
    lane = lax.broadcasted_iota(jnp.int32, (1, 256), 1)
    z = lane & 15
    y = lane >> 4
    out = []
    for dy, dz in OFFSETS:
        ok = (y + dy >= 0) & (y + dy < 16) & (z + dz >= 0) & (z + dz < 16)
        out.append(jnp.where(ok, 1.0, 0.0).astype(jnp.float32))
    return out


def columns(x, masks, sign):
    parts = []
    for i in range(9):
        dy, dz = OFFSETS[i]
        off = sign * (dy * 16 + dz)
        if off == 0:
            parts.append(x)
            continue
        mask = masks[i if sign > 0 else 8 - i]
        parts.append(pltpu.roll(x, (-off) % 256, 1) * mask.astype(x.dtype))
    return jnp.concatenate(parts, axis=0)


def spread(acc, base, width, ys):
    n = len(ys)
    for i in range(n + 2):
        total = None
        for j in range(max(0, i - 2), min(n, i + 1)):
            part = ys[j][width * (i - j) : width * (i - j + 1), :]
            total = part if total is None else total + part
        acc[base + i] = acc[base + i] + total


def full_kernel(
    vox, fl, up, out_r, out_v, out_w,
    xv, uv, wf, wd, accf, accd, accw, far_1, near_1, far_2, near_2, ring, other_w,
    send_sems, recv_sems,
):
    chan = lax.axis_index("chan")
    z = lax.axis_index("filt")
    core = lax.axis_index("space")
    x = lax.rem(chan, 4)
    y = lax.div(chan, 4)

    def target(axis, step):
        if axis == "z":
            return {"filt": lax.rem(z + step + 8, 8)}
        if axis == "x":
            return {"chan": 4 * y + lax.rem(x + step + 4, 4)}
        if axis == "y":
            return {"chan": 4 * lax.rem(y + step + 4, 4) + x}
        return {"space": 1 - core}

    barrier = pltpu.get_barrier_semaphore()
    for axis, step in (("z", 1), ("z", -1), ("x", 1), ("x", -1), ("y", 1), ("y", -1), ("c", 0)):
        pl.semaphore_signal(
            barrier, inc=1, device_id=target(axis, step), device_id_type=pl.DeviceIdType.MESH
        )
    pl.semaphore_wait(barrier, 7)

    copies = []

    def send(source, dest, axis, step):
        k = len(copies)
        copy = pltpu.make_async_remote_copy(
            src_ref=source,
            dst_ref=dest,
            send_sem=send_sems.at[k],
            recv_sem=recv_sems.at[k],
            device_id=target(axis, step),
            device_id_type=pl.DeviceIdType.MESH,
        )
        copy.start()
        copies.append(copy)
        return copy

    steps = (1, -1)
    axes = (("x", "y"), ("y", "x"))
    place = {"x": x, "y": y}

    def block_at(half, first, second):
        a = lax.rem(place[axes[half][0]] + first + 4, 4)
        b = lax.rem(place[axes[half][1]] + second + 4, 4)
        return (4 * b + a) if half == 0 else (4 * a + b)

    def u_at(half, first, second, plane, count):
        return uv.at[pl.ds(1 + 4 * block_at(half, first, second) + 2 * half + plane, count)]

    def v_at(distance, plane, count):
        return xv.at[pl.ds(1 + 8 * lax.rem(z + distance + 8, 8) + plane, count)]

    z_now = [send(vox, v_at(0, 0, 8), "z", st) for st in steps]
    first_sent = [
        [send(up.at[pl.ds(2 * h, 2)], u_at(h, 0, 0, 0, 2), axes[h][0], st) for st in steps]
        for h in range(2)
    ]
    second_sent = {}
    for h in range(2):
        second_sent[h, 0] = [
            send(up.at[pl.ds(2 * h, 2)], u_at(h, 0, 0, 0, 2), axes[h][1], st) for st in steps
        ]

    xv[pl.ds(1 + 8 * z, 8)] = vox[...]
    uv[pl.ds(1 + 4 * chan, 4)] = up[...]
    xv[65 * core] = jnp.zeros((32, 256), jnp.bfloat16)
    uv[65 * core] = jnp.zeros((64, 256), jnp.bfloat16)
    for a in range(3):
        w = fl[9 * a : 9 * a + 9].reshape(288, 64)
        wf[64 * (2 - a) : 64 * (3 - a), :] = w.astype(jnp.float32).T.astype(jnp.bfloat16)
        for t in range(9):
            wd[32 * a : 32 * a + 32, 64 * t : 64 * t + 64] = fl[9 * a + t]
    accf[...] = jnp.zeros_like(accf)
    accd[...] = jnp.zeros_like(accd)
    accw[...] = jnp.zeros_like(accw)
    masks = tap_masks()

    def z_hop(hop, now):
        later = []
        for i, st in enumerate(steps):
            now[i].wait_recv()
            if hop < 3:
                part = v_at(-st * hop, 0, 8)
            elif hop == 3:
                part = v_at(-st * hop, 4 * i, 4)
            else:
                continue
            later.append(send(part, part, "z", st))
        return later

    def pass_second(h, e):
        second_sent[h, e] = [
            send(u_at(h, e, 0, 0, 2), u_at(h, e, 0, 0, 2), axes[h][1], st) for st in steps
        ]

    last = []

    def pass_on(h, e):
        for i, st in enumerate(steps):
            second_sent[h, e][i].wait_recv()
            part = u_at(h, e, -st, i, 1)
            last.append(send(part, part, axes[h][1], st))

    far_sent = [[], []]
    for h in range(2):
        for i, st in enumerate(steps):
            first_sent[h][i].wait_recv()
            part = u_at(h, -st, 0, i, 1)
            far_sent[h].append(send(part, part, axes[h][0], st))
    for h in range(2):
        for e in (-1, 1):
            pass_second(h, e)
    z_now = z_hop(1, z_now)
    for h in range(2):
        pass_on(h, 0)
    for h in range(2):
        for copy in far_sent[h]:
            copy.wait_recv()
        pass_second(h, 2)
    z_now = z_hop(2, z_now)
    for h in range(2):
        pass_on(h, -1)
        pass_on(h, 1)
    z_now = z_hop(3, z_now)
    for h in range(2):
        pass_on(h, 2)
    z_hop(4, z_now)
    for copy in last:
        copy.wait_recv()
    inner, outer = 64 - 63 * core, 65 * core
    halos = [
        send(xv.at[inner], xv.at[outer], "c", 0),
        send(uv.at[inner], uv.at[outer], "c", 0),
    ]

    def forward(b):
        cols = [columns(xv[b * GROUP + j + 1], masks, 1) for j in range(GROUP)]
        ys = [jnp.dot(wf[...], c, preferred_element_type=jnp.float32) for c in cols]
        spread(accf, b * GROUP + 1, 64, ys)
        around = [uv[pl.ds(b * GROUP + j, 3)].reshape(192, 256) for j in range(GROUP)]
        accw[...] = accw[...] + lax.dot_general(
            jnp.concatenate(cols, axis=1),
            jnp.concatenate(around, axis=1),
            (((1,), (1,)), ((), ())),
            preferred_element_type=jnp.float32,
        )

    def backward(b):
        ys = [
            jnp.dot(
                wd[...],
                columns(uv[b * GROUP + j + 1], masks, -1),
                preferred_element_type=jnp.float32,
            )
            for j in range(GROUP)
        ]
        spread(accd, b * GROUP + 1, 32, ys)

    for copy in halos:
        copy.wait_recv()
    for q in (0, 65):
        spread(accf, q, 64, [jnp.dot(wf[...], columns(xv[q], masks, 1), preferred_element_type=jnp.float32)])
        spread(accd, q, 32, [jnp.dot(wd[...], columns(uv[q], masks, -1), preferred_element_type=jnp.float32)])

    @pl.loop(0, 64 // GROUP)
    def _(b):
        forward(b)
        backward(b)

    def d_at(distance, part):
        return accd.at[pl.ds(2 + 8 * lax.rem(z + distance + 8, 8) + 4 * part, 4)]

    ring_sent = [[], []]

    def ring_send(i, j):
        part = (i + j) % 2
        ring_sent[i].append(
            send(d_at(steps[i] * (4 - (j + 1) // 2), part), ring.at[i, j], "z", steps[i])
        )

    def ring_take(j):
        for i in range(2):
            ring_sent[i][j].wait_recv()
            held = d_at(steps[i] * (3 - (j + 1) // 2), (i + j) % 2)
            held[...] = held[...] + ring[i, j]
            if j < 5:
                ring_send(i, j + 2)

    def f_at(half, first, second, plane, count):
        return accf.at[pl.ds(2 + 4 * block_at(1 - half, first, second) + 2 * half + plane, count)]

    far_copies, near_copies = {}, {}

    def far_send(h, d):
        for i, st in enumerate(steps):
            far_copies[h, d, i] = send(
                f_at(h, 2, d, i, 1), far_1.at[h, i, pl.ds(d, 1)], axes[1 - h][0], st
            )

    def far_take(h, d):
        for i, st in enumerate(steps):
            far_copies[h, d, i].wait_recv()
            held = f_at(h, st, d, i, 1)
            held[...] = held[...] + far_1[h, i, pl.ds(d, 1)]
            near_copies[h, d, i] = send(
                f_at(h, st, d, 0, 2), near_1.at[h, i, d], axes[1 - h][0], st
            )

    def near_take(h, d):
        for i in range(2):
            near_copies[h, d, i].wait_recv()
        held = f_at(h, 0, d, 0, 2)
        held[...] = held[...] + near_1[h, 0, d] + near_1[h, 1, d]

    for i in range(2):
        ring_send(i, 0)
        ring_send(i, 1)
    order = (2, 1, 3, 0)
    for d in order:
        for h in range(2):
            far_send(h, d)
    w_copy = send(accw, other_w, "c", 0)
    for j, d in enumerate(order):
        for h in range(2):
            far_take(h, d)
        ring_take(j)
    second_far, second_near = {}, {}
    for h in range(2):
        near_take(h, 2)
        for i, st in enumerate(steps):
            second_far[h, i] = send(
                f_at(h, 0, 2, i, 1), far_2.at[h, pl.ds(i, 1)], axes[1 - h][1], st
            )
    ring_take(4)
    for i, d in ((0, 1), (1, 3)):
        for h in range(2):
            near_take(h, d)
    for i, st in enumerate(steps):
        for h in range(2):
            second_far[h, i].wait_recv()
            held = f_at(h, 0, st, i, 1)
            held[...] = held[...] + far_2[h, pl.ds(i, 1)]
            second_near[h, i] = send(f_at(h, 0, st, 0, 2), near_2.at[h, i], axes[1 - h][1], st)
    ring_take(5)
    for h in range(2):
        near_take(h, 0)
    w_copy.wait_recv()
    other_w[...] = (other_w[...] + accw[...]) / jnp.sqrt(jnp.float32(128 * 256))
    for a in range(3):
        for t in range(9):
            out_w[9 * a + t] = other_w[32 * t : 32 * t + 32, 64 * (2 - a) : 64 * (3 - a)]
    ring_take(6)
    out_v[...] = accd[pl.ds(2 + 8 * z, 8)].astype(jnp.bfloat16)
    for h in range(2):
        for i in range(2):
            second_near[h, i].wait_recv()
        total = f_at(h, 0, 0, 0, 2)[...] + near_2[h, 0] + near_2[h, 1]
        out_r[2 * h : 2 * h + 2] = total.astype(jnp.bfloat16)
    for copy in copies:
        copy.wait_send()


def local(voxels, filters, upstream):
    f32, bf16 = jnp.float32, jnp.bfloat16
    return pl.pallas_call(
        full_kernel,
        out_shape=(
            jax.ShapeDtypeStruct((4, 64, 256), bf16),
            jax.ShapeDtypeStruct((8, 32, 256), bf16),
            jax.ShapeDtypeStruct((27, 32, 64), f32),
        ),
        in_specs=[pl.BlockSpec(memory_space=pltpu.VMEM)] * 3,
        out_specs=[pl.BlockSpec(memory_space=pltpu.VMEM)] * 3,
        scratch_shapes=[
            pltpu.VMEM((66, 32, 256), bf16),
            pltpu.VMEM((66, 64, 256), bf16),
            pltpu.VMEM((192, 288), bf16),
            pltpu.VMEM((96, 576), bf16),
            pltpu.VMEM((68, 64, 256), f32),
            pltpu.VMEM((68, 32, 256), f32),
            pltpu.VMEM((288, 192), f32),
            pltpu.VMEM((2, 2, 4, 64, 256), f32),
            pltpu.VMEM((2, 2, 4, 2, 64, 256), f32),
            pltpu.VMEM((2, 2, 64, 256), f32),
            pltpu.VMEM((2, 2, 2, 64, 256), f32),
            pltpu.VMEM((2, 7, 4, 32, 256), f32),
            pltpu.VMEM((288, 192), f32),
            pltpu.SemaphoreType.DMA((COPIES,)),
            pltpu.SemaphoreType.DMA((COPIES,)),
        ],
        compiler_params=pltpu.CompilerParams(
            collective_id=0, has_side_effects=True, vmem_limit_bytes=60 * 2**20
        ),
    )(voxels, filters, upstream)


def solution(mesh):
    return jax.shard_map(
        local,
        mesh=mesh,
        in_specs=(
            P(("space", "filt"), "chan", None),
            P(None, "chan", "filt"),
            P(("space", "chan"), "filt", None),
        ),
        out_specs=(
            P(("space", "chan"), "filt", None),
            P(("space", "filt"), "chan", None),
            P(None, "chan", "filt"),
        ),
        check_vma=False,
    )
```

```python
import jax
import jax.numpy as jnp
from jax import lax
from jax.experimental import pallas as pl
from jax.experimental.pallas import tpu as pltpu
from jax.sharding import PartitionSpec as P

OFFSETS = [(dy, dz) for dy in (-1, 0, 1) for dz in (-1, 0, 1)]
GROUP = 4
COPIES = 105


def tap_masks():
    lane = lax.broadcasted_iota(jnp.int32, (1, 256), 1)
    z = lane & 15
    y = lane >> 4
    out = []
    for dy, dz in OFFSETS:
        ok = (y + dy >= 0) & (y + dy < 16) & (z + dz >= 0) & (z + dz < 16)
        out.append(jnp.where(ok, 1.0, 0.0).astype(jnp.float32))
    return out


def columns(x, masks, sign):
    parts = []
    for i in range(9):
        dy, dz = OFFSETS[i]
        off = sign * (dy * 16 + dz)
        if off == 0:
            parts.append(x)
            continue
        mask = masks[i if sign > 0 else 8 - i]
        parts.append(pltpu.roll(x, (-off) % 256, 1) * mask.astype(x.dtype))
    return jnp.concatenate(parts, axis=0)


def spread(acc, base, width, ys):
    n = len(ys)
    for i in range(n + 2):
        total = None
        for j in range(max(0, i - 2), min(n, i + 1)):
            part = ys[j][width * (i - j) : width * (i - j + 1), :]
            total = part if total is None else total + part
        acc[base + i] = acc[base + i] + total


def full_kernel(
    vox, fl, up, out_r, out_v, out_w,
    xv, uv, wf, wd, accf, accd, accw, far_1, near_1, far_2, near_2, ring, other_w,
    send_sems, recv_sems,
):
    chan = lax.axis_index("chan")
    z = lax.axis_index("filt")
    core = lax.axis_index("space")
    x = lax.rem(chan, 4)
    y = lax.div(chan, 4)

    def target(axis, step):
        if axis == "z":
            return {"filt": lax.rem(z + step + 8, 8)}
        if axis == "x":
            return {"chan": 4 * y + lax.rem(x + step + 4, 4)}
        if axis == "y":
            return {"chan": 4 * lax.rem(y + step + 4, 4) + x}
        return {"space": 1 - core}

    barrier = pltpu.get_barrier_semaphore()
    for axis, step in (("z", 1), ("z", -1), ("x", 1), ("x", -1), ("y", 1), ("y", -1), ("c", 0)):
        pl.semaphore_signal(
            barrier, inc=1, device_id=target(axis, step), device_id_type=pl.DeviceIdType.MESH
        )
    pl.semaphore_wait(barrier, 7)

    copies = []

    def send(source, dest, axis, step):
        k = len(copies)
        copy = pltpu.make_async_remote_copy(
            src_ref=source,
            dst_ref=dest,
            send_sem=send_sems.at[k],
            recv_sem=recv_sems.at[k],
            device_id=target(axis, step),
            device_id_type=pl.DeviceIdType.MESH,
        )
        copy.start()
        copies.append(copy)
        return copy

    steps = (1, -1)
    axes = (("x", "y"), ("y", "x"))
    place = {"x": x, "y": y}

    def block_at(half, first, second):
        a = lax.rem(place[axes[half][0]] + first + 4, 4)
        b = lax.rem(place[axes[half][1]] + second + 4, 4)
        return (4 * b + a) if half == 0 else (4 * a + b)

    def u_at(half, first, second, plane, count):
        return uv.at[pl.ds(1 + 4 * block_at(half, first, second) + 2 * half + plane, count)]

    def v_at(distance, plane, count):
        return xv.at[pl.ds(1 + 8 * lax.rem(z + distance + 8, 8) + plane, count)]

    z_now = [send(vox, v_at(0, 0, 8), "z", st) for st in steps]
    first_sent = [
        [send(up.at[pl.ds(2 * h, 2)], u_at(h, 0, 0, 0, 2), axes[h][0], st) for st in steps]
        for h in range(2)
    ]
    second_sent = {}
    for h in range(2):
        second_sent[h, 0] = [
            send(up.at[pl.ds(2 * h, 2)], u_at(h, 0, 0, 0, 2), axes[h][1], st) for st in steps
        ]

    xv[pl.ds(1 + 8 * z, 8)] = vox[...]
    uv[pl.ds(1 + 4 * chan, 4)] = up[...]
    xv[65 * core] = jnp.zeros((32, 256), jnp.bfloat16)
    uv[65 * core] = jnp.zeros((64, 256), jnp.bfloat16)
    for a in range(3):
        w = fl[9 * a : 9 * a + 9].reshape(288, 64)
        wf[64 * (2 - a) : 64 * (3 - a), :] = w.astype(jnp.float32).T.astype(jnp.bfloat16)
        for t in range(9):
            wd[32 * a : 32 * a + 32, 64 * t : 64 * t + 64] = fl[9 * a + t]
    accf[...] = jnp.zeros_like(accf)
    accd[...] = jnp.zeros_like(accd)
    accw[...] = jnp.zeros_like(accw)
    masks = tap_masks()

    def z_hop(hop, now):
        later = []
        for i, st in enumerate(steps):
            now[i].wait_recv()
            if hop < 3:
                part = v_at(-st * hop, 0, 8)
            elif hop == 3:
                part = v_at(-st * hop, 4 * i, 4)
            else:
                continue
            later.append(send(part, part, "z", st))
        return later

    def pass_second(h, e):
        second_sent[h, e] = [
            send(u_at(h, e, 0, 0, 2), u_at(h, e, 0, 0, 2), axes[h][1], st) for st in steps
        ]

    last = []

    def pass_on(h, e):
        for i, st in enumerate(steps):
            second_sent[h, e][i].wait_recv()
            part = u_at(h, e, -st, i, 1)
            last.append(send(part, part, axes[h][1], st))

    def forward(p0):
        ys = [
            jnp.dot(wf[...], columns(xv[p0 + j], masks, 1), preferred_element_type=jnp.float32)
            for j in range(8)
        ]
        spread(accf, p0, 64, ys)

    def backward(starts):
        found = [
            [
                jnp.dot(
                    wd[...], columns(uv[p0 + j], masks, -1), preferred_element_type=jnp.float32
                )
                for j in range(4)
            ]
            for p0 in starts
        ]
        for p0, ys in zip(starts, found):
            spread(accd, p0, 32, ys)

    def forward_at(hop):
        @pl.loop(0, 2)
        def _(k):
            forward(1 + 8 * lax.rem(z + hop * (1 - 2 * k) + 8, 8))

    def u_start(dx, dy):
        return 1 + 4 * (4 * lax.rem(y + dy + 4, 4) + lax.rem(x + dx + 4, 4))

    def weights(low, high):
        @pl.loop(low, high)
        def _(b):
            cols = [columns(xv[b * GROUP + j + 1], masks, 1) for j in range(GROUP)]
            around = [uv[pl.ds(b * GROUP + j, 3)].reshape(192, 256) for j in range(GROUP)]
            accw[...] = accw[...] + lax.dot_general(
                jnp.concatenate(cols, axis=1),
                jnp.concatenate(around, axis=1),
                (((1,), (1,)), ((), ())),
                preferred_element_type=jnp.float32,
            )

    far_sent = [[], []]
    for h in range(2):
        for i, st in enumerate(steps):
            first_sent[h][i].wait_recv()
            part = u_at(h, -st, 0, i, 1)
            far_sent[h].append(send(part, part, axes[h][0], st))
    for h in range(2):
        for e in (-1, 1):
            pass_second(h, e)
    forward(1 + 8 * z)
    z_now = z_hop(1, z_now)
    for h in range(2):
        pass_on(h, 0)
    for h in range(2):
        for copy in far_sent[h]:
            copy.wait_recv()
        pass_second(h, 2)
    forward_at(1)
    z_now = z_hop(2, z_now)
    for h in range(2):
        pass_on(h, -1)
        pass_on(h, 1)
    backward([u_start(0, 0)])

    @pl.loop(0, 2)
    def _(k):
        backward([u_start(1 - 2 * k, 0), u_start(0, 1 - 2 * k)])

    forward_at(2)
    z_now = z_hop(3, z_now)
    for h in range(2):
        pass_on(h, 2)
    forward_at(3)

    @pl.loop(0, 2)
    def _(k):
        backward([u_start(1 - 2 * k, 1), u_start(1 - 2 * k, -1)])

    z_hop(4, z_now)
    inner, outer = 64 - 63 * core, 65 * core
    x_halo = send(xv.at[inner], xv.at[outer], "c", 0)
    forward(1 + 8 * lax.rem(z + 4, 8))
    for copy in last:
        copy.wait_recv()
    u_halo = send(uv.at[inner], uv.at[outer], "c", 0)
    x_halo.wait_recv()
    for q in (0, 65):
        spread(accf, q, 64, [jnp.dot(wf[...], columns(xv[q], masks, 1), preferred_element_type=jnp.float32)])

    def d_at(distance, part):
        return accd.at[pl.ds(2 + 8 * lax.rem(z + distance + 8, 8) + 4 * part, 4)]

    ring_sent = [[], []]

    def ring_send(i, j):
        part = (i + j) % 2
        ring_sent[i].append(
            send(d_at(steps[i] * (4 - (j + 1) // 2), part), ring.at[i, j], "z", steps[i])
        )

    def ring_take(j):
        for i in range(2):
            ring_sent[i][j].wait_recv()
            held = d_at(steps[i] * (3 - (j + 1) // 2), (i + j) % 2)
            held[...] = held[...] + ring[i, j]
            if j < 5:
                ring_send(i, j + 2)

    def f_at(half, first, second, plane, count):
        return accf.at[pl.ds(2 + 4 * block_at(1 - half, first, second) + 2 * half + plane, count)]

    far_copies, near_copies = {}, {}

    def far_send(h, d):
        for i, st in enumerate(steps):
            far_copies[h, d, i] = send(
                f_at(h, 2, d, i, 1), far_1.at[h, i, pl.ds(d, 1)], axes[1 - h][0], st
            )

    def far_take(h, d):
        for i, st in enumerate(steps):
            far_copies[h, d, i].wait_recv()
            held = f_at(h, st, d, i, 1)
            held[...] = held[...] + far_1[h, i, pl.ds(d, 1)]
            near_copies[h, d, i] = send(
                f_at(h, st, d, 0, 2), near_1.at[h, i, d], axes[1 - h][0], st
            )

    def near_take(h, d):
        for i in range(2):
            near_copies[h, d, i].wait_recv()
        held = f_at(h, 0, d, 0, 2)
        held[...] = held[...] + near_1[h, 0, d] + near_1[h, 1, d]

    order = (2, 1, 3, 0)
    for d in order:
        for h in range(2):
            far_send(h, d)

    @pl.loop(0, 3)
    def _(k):
        t = k + lax.div(k, 2)
        backward([u_start(2, t), u_start(t, 2)])

    backward([u_start(2, 2)])
    u_halo.wait_recv()
    for q in (0, 65):
        spread(accd, q, 32, [jnp.dot(wd[...], columns(uv[q], masks, -1), preferred_element_type=jnp.float32)])
    for i in range(2):
        ring_send(i, 0)
        ring_send(i, 1)
    for d, low in ((2, 0), (1, 0), (3, 2), (0, 4)):
        for h in range(2):
            far_take(h, d)
        if d != 2:
            weights(low, low + 2)
    ring_take(0)
    second_far, second_near = {}, {}
    for h in range(2):
        near_take(h, 2)
        for i, st in enumerate(steps):
            second_far[h, i] = send(
                f_at(h, 0, 2, i, 1), far_2.at[h, pl.ds(i, 1)], axes[1 - h][1], st
            )
    weights(6, 9)
    ring_take(1)
    for h in range(2):
        near_take(h, 1)
    weights(9, 12)
    ring_take(2)
    for h in range(2):
        near_take(h, 3)
    for i, st in enumerate(steps):
        for h in range(2):
            second_far[h, i].wait_recv()
            held = f_at(h, 0, st, i, 1)
            held[...] = held[...] + far_2[h, pl.ds(i, 1)]
            second_near[h, i] = send(f_at(h, 0, st, 0, 2), near_2.at[h, i], axes[1 - h][1], st)
    weights(12, 16)
    w_copy = send(accw, other_w, "c", 0)
    ring_take(3)
    for h in range(2):
        near_take(h, 0)
    ring_take(4)
    w_copy.wait_recv()
    other_w[...] = (other_w[...] + accw[...]) / jnp.sqrt(jnp.float32(128 * 256))
    for a in range(3):
        for t in range(9):
            out_w[9 * a + t] = other_w[32 * t : 32 * t + 32, 64 * (2 - a) : 64 * (3 - a)]
    ring_take(5)
    for h in range(2):
        for i in range(2):
            second_near[h, i].wait_recv()
        total = f_at(h, 0, 0, 0, 2)[...] + near_2[h, 0] + near_2[h, 1]
        out_r[2 * h : 2 * h + 2] = total.astype(jnp.bfloat16)
    ring_take(6)
    out_v[...] = accd[pl.ds(2 + 8 * z, 8)].astype(jnp.bfloat16)
    for copy in copies:
        copy.wait_send()


def local(voxels, filters, upstream):
    f32, bf16 = jnp.float32, jnp.bfloat16
    return pl.pallas_call(
        full_kernel,
        out_shape=(
            jax.ShapeDtypeStruct((4, 64, 256), bf16),
            jax.ShapeDtypeStruct((8, 32, 256), bf16),
            jax.ShapeDtypeStruct((27, 32, 64), f32),
        ),
        in_specs=[pl.BlockSpec(memory_space=pltpu.VMEM)] * 3,
        out_specs=[pl.BlockSpec(memory_space=pltpu.VMEM)] * 3,
        scratch_shapes=[
            pltpu.VMEM((66, 32, 256), bf16),
            pltpu.VMEM((66, 64, 256), bf16),
            pltpu.VMEM((192, 288), bf16),
            pltpu.VMEM((96, 576), bf16),
            pltpu.VMEM((68, 64, 256), f32),
            pltpu.VMEM((68, 32, 256), f32),
            pltpu.VMEM((288, 192), f32),
            pltpu.VMEM((2, 2, 4, 64, 256), f32),
            pltpu.VMEM((2, 2, 4, 2, 64, 256), f32),
            pltpu.VMEM((2, 2, 64, 256), f32),
            pltpu.VMEM((2, 2, 2, 64, 256), f32),
            pltpu.VMEM((2, 7, 4, 32, 256), f32),
            pltpu.VMEM((288, 192), f32),
            pltpu.SemaphoreType.DMA((COPIES,)),
            pltpu.SemaphoreType.DMA((COPIES,)),
        ],
        compiler_params=pltpu.CompilerParams(
            collective_id=0, has_side_effects=True, vmem_limit_bytes=60 * 2**20
        ),
    )(voxels, filters, upstream)


def solution(mesh):
    return jax.shard_map(
        local,
        mesh=mesh,
        in_specs=(
            P(("space", "filt"), "chan", None),
            P(None, "chan", "filt"),
            P(("space", "chan"), "filt", None),
        ),
        out_specs=(
            P(("space", "chan"), "filt", None),
            P(("space", "filt"), "chan", None),
            P(None, "chan", "filt"),
        ),
        check_vma=False,
    )
```

```python
import jax
import jax.numpy as jnp
from jax import lax
from jax.experimental import pallas as pl
from jax.experimental.pallas import tpu as pltpu
from jax.sharding import PartitionSpec as P

OFFSETS = [(dy, dz) for dy in (-1, 0, 1) for dz in (-1, 0, 1)]
GROUP = 4
COPIES = 145


def tap_masks():
    lane = lax.broadcasted_iota(jnp.int32, (1, 256), 1)
    z = lane & 15
    y = lane >> 4
    out = []
    for dy, dz in OFFSETS:
        ok = (y + dy >= 0) & (y + dy < 16) & (z + dz >= 0) & (z + dz < 16)
        out.append(jnp.where(ok, 1.0, 0.0).astype(jnp.float32))
    return out


def columns(x, masks, sign):
    parts = []
    for i in range(9):
        dy, dz = OFFSETS[i]
        off = sign * (dy * 16 + dz)
        if off == 0:
            parts.append(x)
            continue
        mask = masks[i if sign > 0 else 8 - i]
        parts.append(pltpu.roll(x, (-off) % 256, 1) * mask.astype(x.dtype))
    return jnp.concatenate(parts, axis=0)


def spread(acc, base, width, ys):
    n = len(ys)
    for i in range(n + 2):
        total = None
        for j in range(max(0, i - 2), min(n, i + 1)):
            part = ys[j][width * (i - j) : width * (i - j + 1), :]
            total = part if total is None else total + part
        acc[base + i] = acc[base + i] + total


def full_kernel(
    vox, fl, up, out_r, out_v, out_w,
    xv, uv, wf, wd, accf, accd, accw, far_1, near_1, far_2, near_2, ring, other_w,
    send_sems, recv_sems,
):
    chan = lax.axis_index("chan")
    z = lax.axis_index("filt")
    core = lax.axis_index("space")
    x = lax.rem(chan, 4)
    y = lax.div(chan, 4)

    def target(axis, step):
        if axis == "z":
            return {"filt": lax.rem(z + step + 8, 8)}
        if axis == "x":
            return {"chan": 4 * y + lax.rem(x + step + 4, 4)}
        if axis == "y":
            return {"chan": 4 * lax.rem(y + step + 4, 4) + x}
        return {"space": 1 - core}

    barrier = pltpu.get_barrier_semaphore()
    for axis, step in (("z", 1), ("z", -1), ("x", 1), ("x", -1), ("y", 1), ("y", -1), ("c", 0)):
        pl.semaphore_signal(
            barrier, inc=1, device_id=target(axis, step), device_id_type=pl.DeviceIdType.MESH
        )
    pl.semaphore_wait(barrier, 7)

    copies = []

    def send(source, dest, axis, step):
        k = len(copies)
        copy = pltpu.make_async_remote_copy(
            src_ref=source,
            dst_ref=dest,
            send_sem=send_sems.at[k],
            recv_sem=recv_sems.at[k],
            device_id=target(axis, step),
            device_id_type=pl.DeviceIdType.MESH,
        )
        copy.start()
        copies.append(copy)
        return copy

    steps = (1, -1)
    axes = (("x", "y"), ("y", "x"))
    place = {"x": x, "y": y}

    def block_at(half, first, second):
        a = lax.rem(place[axes[half][0]] + first + 4, 4)
        b = lax.rem(place[axes[half][1]] + second + 4, 4)
        return (4 * b + a) if half == 0 else (4 * a + b)

    def u_at(half, first, second, plane, count):
        return uv.at[pl.ds(1 + 4 * block_at(half, first, second) + 2 * half + plane, count)]

    def v_at(distance, plane, count):
        return xv.at[pl.ds(1 + 8 * lax.rem(z + distance + 8, 8) + plane, count)]

    first_sent, second_sent = {}, {}
    for turn in range(2):
        for h in range(2):
            for i, st in enumerate(steps):
                n = (i + turn) % 2
                first_sent[h, i, n] = send(
                    up.at[pl.ds(2 * h + n, 1)], u_at(h, 0, 0, n, 1), axes[h][0], st
                )
    z_sent = {}
    for n in range(4):
        for i, st in enumerate(steps):
            part = n if i == 0 else 3 - n
            z_sent[1, i, n] = send(vox.at[pl.ds(2 * part, 2)], v_at(0, 2 * part, 2), "z", st)
    for turn in range(2):
        for h in range(2):
            for i, st in enumerate(steps):
                n = (i + turn) % 2
                second_sent[h, 0, i, n] = send(
                    up.at[pl.ds(2 * h + n, 1)], u_at(h, 0, 0, n, 1), axes[h][1], st
                )

    xv[pl.ds(1 + 8 * z, 8)] = vox[...]
    uv[pl.ds(1 + 4 * chan, 4)] = up[...]
    xv[65 * core] = jnp.zeros((32, 256), jnp.bfloat16)
    uv[65 * core] = jnp.zeros((64, 256), jnp.bfloat16)
    for a in range(3):
        w = fl[9 * a : 9 * a + 9].reshape(288, 64)
        wf[64 * (2 - a) : 64 * (3 - a), :] = w.astype(jnp.float32).T.astype(jnp.bfloat16)
        for t in range(9):
            wd[32 * a : 32 * a + 32, 64 * t : 64 * t + 64] = fl[9 * a + t]
    accf[...] = jnp.zeros_like(accf)
    accd[...] = jnp.zeros_like(accd)
    accw[...] = jnp.zeros_like(accw)
    masks = tap_masks()

    def z_hop(hop, pieces):
        for n in pieces:
            for i, st in enumerate(steps):
                if hop == 4 and n > 1:
                    continue
                z_sent[hop, i, n].wait_recv()
                if hop == 4 or (hop == 3 and n > 1):
                    continue
                piece = v_at(-st * hop, 2 * (n if i == 0 else 3 - n), 2)
                z_sent[hop + 1, i, n] = send(piece, piece, "z", st)

    def pass_second(h, e):
        for turn in range(2):
            for i, st in enumerate(steps):
                n = (i + turn) % 2
                part = u_at(h, e, 0, n, 1)
                second_sent[h, e, i, n] = send(part, part, axes[h][1], st)

    last = []

    def pass_on(h, e):
        for i, st in enumerate(steps):
            second_sent[h, e, i, i].wait_recv()
            part = u_at(h, e, -st, i, 1)
            last.append(send(part, part, axes[h][1], st))

    def rest_of(h, e):
        for i in range(2):
            second_sent[h, e, i, 1 - i].wait_recv()

    def forward(p0):
        ys = [
            jnp.dot(wf[...], columns(xv[p0 + j], masks, 1), preferred_element_type=jnp.float32)
            for j in range(8)
        ]
        spread(accf, p0, 64, ys)

    def backward(starts):
        found = [
            [
                jnp.dot(
                    wd[...], columns(uv[p0 + j], masks, -1), preferred_element_type=jnp.float32
                )
                for j in range(4)
            ]
            for p0 in starts
        ]
        for p0, ys in zip(starts, found):
            spread(accd, p0, 32, ys)

    def forward_at(hop):
        @pl.loop(0, 2)
        def _(k):
            forward(1 + 8 * lax.rem(z + hop * (1 - 2 * k) + 8, 8))

    def u_start(dx, dy):
        return 1 + 4 * (4 * lax.rem(y + dy + 4, 4) + lax.rem(x + dx + 4, 4))

    def weights(low, high):
        @pl.loop(low, high)
        def _(b):
            cols = [columns(xv[b * GROUP + j + 1], masks, 1) for j in range(GROUP)]
            around = [uv[pl.ds(b * GROUP + j, 3)].reshape(192, 256) for j in range(GROUP)]
            accw[...] = accw[...] + lax.dot_general(
                jnp.concatenate(cols, axis=1),
                jnp.concatenate(around, axis=1),
                (((1,), (1,)), ((), ())),
                preferred_element_type=jnp.float32,
            )

    far_sent = [[], []]
    for h in range(2):
        for i, st in enumerate(steps):
            first_sent[h, i, i].wait_recv()
            part = u_at(h, -st, 0, i, 1)
            far_sent[h].append(send(part, part, axes[h][0], st))
    for h in range(2):
        for i in range(2):
            first_sent[h, i, 1 - i].wait_recv()
    for h in range(2):
        pass_second(h, -1)
        pass_second(h, 1)
    z_hop(1, (0, 1))
    for h in range(2):
        pass_on(h, 0)
    z_hop(1, (2, 3))
    forward(1 + 8 * z)
    for h in range(2):
        for copy in far_sent[h]:
            copy.wait_recv()
        pass_second(h, 2)
    z_hop(2, (0, 1))
    forward(1 + 8 * lax.rem(z + 1, 8))
    z_hop(2, (2, 3))
    for h in range(2):
        pass_on(h, -1)
    forward(1 + 8 * lax.rem(z + 7, 8))
    z_hop(3, (0, 1))
    for h in range(2):
        pass_on(h, 1)
    forward(1 + 8 * lax.rem(z + 2, 8))
    z_hop(3, (2, 3))
    for h in range(2):
        pass_on(h, 2)
    forward(1 + 8 * lax.rem(z + 6, 8))
    forward_at(3)
    z_hop(4, (0, 1))
    inner, outer = 64 - 63 * core, 65 * core
    x_halo = send(xv.at[inner], xv.at[outer], "c", 0)
    forward(1 + 8 * lax.rem(z + 4, 8))
    for h in range(2):
        rest_of(h, 0)
    backward([u_start(0, 0)])

    @pl.loop(0, 2)
    def _(k):
        backward([u_start(1 - 2 * k, 0), u_start(0, 1 - 2 * k)])

    for h in range(2):
        for e in (-1, 1, 2):
            rest_of(h, e)
    for copy in last:
        copy.wait_recv()
    u_halo = send(uv.at[inner], uv.at[outer], "c", 0)
    x_halo.wait_recv()
    for q in (0, 65):
        spread(accf, q, 64, [jnp.dot(wf[...], columns(xv[q], masks, 1), preferred_element_type=jnp.float32)])

    def d_at(distance, part):
        return accd.at[pl.ds(2 + 8 * lax.rem(z + distance + 8, 8) + 4 * part, 4)]

    ring_sent = [[], []]

    def ring_send(i, j):
        part = (i + j) % 2
        ring_sent[i].append(
            send(d_at(steps[i] * (4 - (j + 1) // 2), part), ring.at[i, j], "z", steps[i])
        )

    def ring_take(j):
        for i in range(2):
            ring_sent[i][j].wait_recv()
            held = d_at(steps[i] * (3 - (j + 1) // 2), (i + j) % 2)
            held[...] = held[...] + ring[i, j]
            if j < 5:
                ring_send(i, j + 2)

    def f_at(half, first, second, plane, count):
        return accf.at[pl.ds(2 + 4 * block_at(1 - half, first, second) + 2 * half + plane, count)]

    far_copies, near_copies = {}, {}

    def far_send(h, d):
        for i, st in enumerate(steps):
            far_copies[h, d, i] = send(
                f_at(h, 2, d, i, 1), far_1.at[h, i, pl.ds(d, 1)], axes[1 - h][0], st
            )

    def far_take(h, d):
        for i, st in enumerate(steps):
            far_copies[h, d, i].wait_recv()
            held = f_at(h, st, d, i, 1)
            held[...] = held[...] + far_1[h, i, pl.ds(d, 1)]
            near_copies[h, d, i] = send(
                f_at(h, st, d, 0, 2), near_1.at[h, i, d], axes[1 - h][0], st
            )

    def near_take(h, d):
        for i in range(2):
            near_copies[h, d, i].wait_recv()
        held = f_at(h, 0, d, 0, 2)
        held[...] = held[...] + near_1[h, 0, d] + near_1[h, 1, d]

    order = (2, 1, 3, 0)
    for d in order:
        for h in range(2):
            far_send(h, d)

    @pl.loop(0, 2)
    def _(k):
        backward([u_start(1 - 2 * k, 1), u_start(1 - 2 * k, -1)])

    for h in range(2):
        far_take(h, 2)

    @pl.loop(0, 3)
    def _(k):
        t = k + lax.div(k, 2)
        backward([u_start(2, t), u_start(t, 2)])

    backward([u_start(2, 2)])
    u_halo.wait_recv()
    for q in (0, 65):
        spread(accd, q, 32, [jnp.dot(wd[...], columns(uv[q], masks, -1), preferred_element_type=jnp.float32)])
    for i in range(2):
        ring_send(i, 0)
        ring_send(i, 1)
    for d in (1, 3):
        for h in range(2):
            far_take(h, d)
    weights(0, 2)
    second_far, second_near = {}, {}
    for h in range(2):
        near_take(h, 2)
        for i, st in enumerate(steps):
            second_far[h, i] = send(
                f_at(h, 0, 2, i, 1), far_2.at[h, pl.ds(i, 1)], axes[1 - h][1], st
            )
    for h in range(2):
        far_take(h, 0)
    ring_take(0)
    weights(2, 6)
    weights(6, 9)
    ring_take(1)
    for h in range(2):
        near_take(h, 1)
    weights(9, 12)
    ring_take(2)
    for h in range(2):
        near_take(h, 3)
    for i, st in enumerate(steps):
        for h in range(2):
            second_far[h, i].wait_recv()
            held = f_at(h, 0, st, i, 1)
            held[...] = held[...] + far_2[h, pl.ds(i, 1)]
            second_near[h, i] = send(f_at(h, 0, st, 0, 2), near_2.at[h, i], axes[1 - h][1], st)
    weights(12, 16)
    w_copy = send(accw, other_w, "c", 0)
    ring_take(3)
    for h in range(2):
        near_take(h, 0)
    ring_take(4)
    w_copy.wait_recv()
    other_w[...] = (other_w[...] + accw[...]) / jnp.sqrt(jnp.float32(128 * 256))
    for a in range(3):
        for t in range(9):
            out_w[9 * a + t] = other_w[32 * t : 32 * t + 32, 64 * (2 - a) : 64 * (3 - a)]
    ring_take(5)
    for h in range(2):
        for i in range(2):
            second_near[h, i].wait_recv()
        total = f_at(h, 0, 0, 0, 2)[...] + near_2[h, 0] + near_2[h, 1]
        out_r[2 * h : 2 * h + 2] = total.astype(jnp.bfloat16)
    ring_take(6)
    out_v[...] = accd[pl.ds(2 + 8 * z, 8)].astype(jnp.bfloat16)
    for copy in copies:
        copy.wait_send()


def local(voxels, filters, upstream):
    f32, bf16 = jnp.float32, jnp.bfloat16
    return pl.pallas_call(
        full_kernel,
        out_shape=(
            jax.ShapeDtypeStruct((4, 64, 256), bf16),
            jax.ShapeDtypeStruct((8, 32, 256), bf16),
            jax.ShapeDtypeStruct((27, 32, 64), f32),
        ),
        in_specs=[pl.BlockSpec(memory_space=pltpu.VMEM)] * 3,
        out_specs=[pl.BlockSpec(memory_space=pltpu.VMEM)] * 3,
        scratch_shapes=[
            pltpu.VMEM((66, 32, 256), bf16),
            pltpu.VMEM((66, 64, 256), bf16),
            pltpu.VMEM((192, 288), bf16),
            pltpu.VMEM((96, 576), bf16),
            pltpu.VMEM((68, 64, 256), f32),
            pltpu.VMEM((68, 32, 256), f32),
            pltpu.VMEM((288, 192), f32),
            pltpu.VMEM((2, 2, 4, 64, 256), f32),
            pltpu.VMEM((2, 2, 4, 2, 64, 256), f32),
            pltpu.VMEM((2, 2, 64, 256), f32),
            pltpu.VMEM((2, 2, 2, 64, 256), f32),
            pltpu.VMEM((2, 7, 4, 32, 256), f32),
            pltpu.VMEM((288, 192), f32),
            pltpu.SemaphoreType.DMA((COPIES,)),
            pltpu.SemaphoreType.DMA((COPIES,)),
        ],
        compiler_params=pltpu.CompilerParams(
            collective_id=0, has_side_effects=True, vmem_limit_bytes=60 * 2**20
        ),
    )(voxels, filters, upstream)


def solution(mesh):
    return jax.shard_map(
        local,
        mesh=mesh,
        in_specs=(
            P(("space", "filt"), "chan", None),
            P(None, "chan", "filt"),
            P(("space", "chan"), "filt", None),
        ),
        out_specs=(
            P(("space", "chan"), "filt", None),
            P(("space", "filt"), "chan", None),
            P(None, "chan", "filt"),
        ),
        check_vma=False,
    )
```

```python
import jax
import jax.numpy as jnp
from jax import lax
from jax.experimental import pallas as pl
from jax.experimental.pallas import tpu as pltpu
from jax.sharding import PartitionSpec as P

OFFSETS = [(dy, dz) for dy in (-1, 0, 1) for dz in (-1, 0, 1)]
GROUP = 4
COPIES = 145


def tap_masks():
    lane = lax.broadcasted_iota(jnp.int32, (1, 256), 1)
    z = lane & 15
    y = lane >> 4
    out = []
    for dy, dz in OFFSETS:
        ok = (y + dy >= 0) & (y + dy < 16) & (z + dz >= 0) & (z + dz < 16)
        out.append(jnp.where(ok, 1.0, 0.0).astype(jnp.float32))
    return out


def columns(x, masks, sign):
    parts = []
    for i in range(9):
        dy, dz = OFFSETS[i]
        off = sign * (dy * 16 + dz)
        if off == 0:
            parts.append(x)
            continue
        mask = masks[i if sign > 0 else 8 - i]
        parts.append(pltpu.roll(x, (-off) % 256, 1) * mask.astype(x.dtype))
    return jnp.concatenate(parts, axis=0)


def spread(acc, base, width, ys):
    n = len(ys)
    for i in range(n + 2):
        total = None
        for j in range(max(0, i - 2), min(n, i + 1)):
            part = ys[j][width * (i - j) : width * (i - j + 1), :]
            total = part if total is None else total + part
        acc[base + i] = acc[base + i] + total


def full_kernel(
    vox, fl, up, out_r, out_v, out_w,
    xv, uv, wf, wd, accf, accd, accw, far_1, near_1, far_2, near_2, ring, other_w,
    send_sems, recv_sems,
):
    chan = lax.axis_index("chan")
    z = lax.axis_index("filt")
    core = lax.axis_index("space")
    x = lax.rem(chan, 4)
    y = lax.div(chan, 4)

    def target(axis, step):
        if axis == "z":
            return {"filt": lax.rem(z + step + 8, 8)}
        if axis == "x":
            return {"chan": 4 * y + lax.rem(x + step + 4, 4)}
        if axis == "y":
            return {"chan": 4 * lax.rem(y + step + 4, 4) + x}
        return {"space": 1 - core}

    barrier = pltpu.get_barrier_semaphore()
    for axis, step in (("z", 1), ("z", -1), ("x", 1), ("x", -1), ("y", 1), ("y", -1), ("c", 0)):
        pl.semaphore_signal(
            barrier, inc=1, device_id=target(axis, step), device_id_type=pl.DeviceIdType.MESH
        )
    pl.semaphore_wait(barrier, 7)

    copies = []

    def send(source, dest, axis, step):
        k = len(copies)
        copy = pltpu.make_async_remote_copy(
            src_ref=source,
            dst_ref=dest,
            send_sem=send_sems.at[k],
            recv_sem=recv_sems.at[k],
            device_id=target(axis, step),
            device_id_type=pl.DeviceIdType.MESH,
        )
        copy.start()
        copies.append(copy)
        return copy

    steps = (1, -1)
    axes = (("x", "y"), ("y", "x"))
    place = {"x": x, "y": y}

    def block_at(half, first, second):
        a = lax.rem(place[axes[half][0]] + first + 4, 4)
        b = lax.rem(place[axes[half][1]] + second + 4, 4)
        return (4 * b + a) if half == 0 else (4 * a + b)

    def u_at(half, first, second, plane, count):
        return uv.at[pl.ds(1 + 4 * block_at(half, first, second) + 2 * half + plane, count)]

    def v_at(distance, plane, count):
        return xv.at[pl.ds(1 + 8 * lax.rem(z + distance + 8, 8) + plane, count)]

    first_sent, second_sent = {}, {}
    for turn in range(2):
        for h in range(2):
            for i, st in enumerate(steps):
                n = (i + turn) % 2
                first_sent[h, i, n] = send(
                    up.at[pl.ds(2 * h + n, 1)], u_at(h, 0, 0, n, 1), axes[h][0], st
                )
    z_sent = {}
    for n in range(4):
        for i, st in enumerate(steps):
            part = n if i == 0 else 3 - n
            z_sent[1, i, n] = send(vox.at[pl.ds(2 * part, 2)], v_at(0, 2 * part, 2), "z", st)
    for turn in range(2):
        for h in range(2):
            for i, st in enumerate(steps):
                n = (i + turn) % 2
                second_sent[h, 0, i, n] = send(
                    up.at[pl.ds(2 * h + n, 1)], u_at(h, 0, 0, n, 1), axes[h][1], st
                )

    xv[pl.ds(1 + 8 * z, 8)] = vox[...]
    uv[pl.ds(1 + 4 * chan, 4)] = up[...]
    xv[65 * core] = jnp.zeros((32, 256), jnp.bfloat16)
    uv[65 * core] = jnp.zeros((64, 256), jnp.bfloat16)
    for a in range(3):
        w = fl[9 * a : 9 * a + 9].reshape(288, 64)
        wf[64 * (2 - a) : 64 * (3 - a), :] = w.astype(jnp.float32).T.astype(jnp.bfloat16)
        for t in range(9):
            wd[32 * a : 32 * a + 32, 64 * t : 64 * t + 64] = fl[9 * a + t]
    accf[...] = jnp.zeros_like(accf)
    accd[...] = jnp.zeros_like(accd)
    accw[...] = jnp.zeros_like(accw)
    masks = tap_masks()

    def z_hop(hop, pieces):
        for n in pieces:
            for i, st in enumerate(steps):
                if hop == 4 and n > 1:
                    continue
                z_sent[hop, i, n].wait_recv()
                if hop == 4 or (hop == 3 and n > 1):
                    continue
                piece = v_at(-st * hop, 2 * (n if i == 0 else 3 - n), 2)
                z_sent[hop + 1, i, n] = send(piece, piece, "z", st)

    def pass_second(h, e):
        for turn in range(2):
            for i, st in enumerate(steps):
                n = (i + turn) % 2
                part = u_at(h, e, 0, n, 1)
                second_sent[h, e, i, n] = send(part, part, axes[h][1], st)

    last = []

    def pass_on(h, e):
        for i, st in enumerate(steps):
            second_sent[h, e, i, i].wait_recv()
            part = u_at(h, e, -st, i, 1)
            last.append(send(part, part, axes[h][1], st))

    def rest_of(h, e):
        for i in range(2):
            second_sent[h, e, i, 1 - i].wait_recv()

    def forward(p0):
        ys = [
            jnp.dot(wf[...], columns(xv[p0 + j], masks, 1), preferred_element_type=jnp.float32)
            for j in range(8)
        ]
        spread(accf, p0, 64, ys)

    def backward(starts):
        found = [
            [
                jnp.dot(
                    wd[...], columns(uv[p0 + j], masks, -1), preferred_element_type=jnp.float32
                )
                for j in range(4)
            ]
            for p0 in starts
        ]
        for p0, ys in zip(starts, found):
            spread(accd, p0, 32, ys)

    def forward_at(hop):
        @pl.loop(0, 2)
        def _(k):
            forward(1 + 8 * lax.rem(z + hop * (1 - 2 * k) + 8, 8))

    def u_start(dx, dy):
        return 1 + 4 * (4 * lax.rem(y + dy + 4, 4) + lax.rem(x + dx + 4, 4))

    def weights(low, high):
        @pl.loop(low, high)
        def _(b):
            cols = [columns(xv[b * GROUP + j + 1], masks, 1) for j in range(GROUP)]
            around = [uv[pl.ds(b * GROUP + j, 3)].reshape(192, 256) for j in range(GROUP)]
            accw[...] = accw[...] + lax.dot_general(
                jnp.concatenate(cols, axis=1),
                jnp.concatenate(around, axis=1),
                (((1,), (1,)), ((), ())),
                preferred_element_type=jnp.float32,
            )

    far_sent = [[], []]
    for h in range(2):
        for i, st in enumerate(steps):
            first_sent[h, i, i].wait_recv()
            part = u_at(h, -st, 0, i, 1)
            far_sent[h].append(send(part, part, axes[h][0], st))
    for h in range(2):
        for i in range(2):
            first_sent[h, i, 1 - i].wait_recv()
    for h in range(2):
        pass_second(h, -1)
        pass_second(h, 1)
    z_hop(1, (0, 1))
    for h in range(2):
        pass_on(h, 0)
    z_hop(1, (2, 3))
    forward(1 + 8 * z)
    for h in range(2):
        for copy in far_sent[h]:
            copy.wait_recv()
        pass_second(h, 2)
    z_hop(2, (0, 1))
    forward(1 + 8 * lax.rem(z + 1, 8))
    z_hop(2, (2, 3))
    for h in range(2):
        pass_on(h, -1)
    forward(1 + 8 * lax.rem(z + 7, 8))
    z_hop(3, (0, 1))
    for h in range(2):
        pass_on(h, 1)
    forward(1 + 8 * lax.rem(z + 2, 8))
    z_hop(3, (2, 3))
    for h in range(2):
        pass_on(h, 2)
    forward(1 + 8 * lax.rem(z + 6, 8))
    forward_at(3)
    z_hop(4, (0, 1))
    inner, outer = 64 - 63 * core, 65 * core
    x_halo = send(xv.at[inner], xv.at[outer], "c", 0)
    forward(1 + 8 * lax.rem(z + 4, 8))
    for h in range(2):
        rest_of(h, 0)
    backward([u_start(0, 0)])

    @pl.loop(0, 2)
    def _(k):
        backward([u_start(1 - 2 * k, 0), u_start(0, 1 - 2 * k)])

    for h in range(2):
        for e in (-1, 1, 2):
            rest_of(h, e)
    for copy in last:
        copy.wait_recv()
    u_halo = send(uv.at[inner], uv.at[outer], "c", 0)
    x_halo.wait_recv()
    for q in (0, 65):
        spread(accf, q, 64, [jnp.dot(wf[...], columns(xv[q], masks, 1), preferred_element_type=jnp.float32)])

    def d_at(distance, part):
        return accd.at[pl.ds(2 + 8 * lax.rem(z + distance + 8, 8) + 4 * part, 4)]

    ring_sent = [[], []]

    def ring_send(i, j):
        part = (i + j) % 2
        ring_sent[i].append(
            send(d_at(steps[i] * (4 - (j + 1) // 2), part), ring.at[i, j], "z", steps[i])
        )

    def ring_take(j):
        for i in range(2):
            ring_sent[i][j].wait_recv()
            held = d_at(steps[i] * (3 - (j + 1) // 2), (i + j) % 2)
            held[...] = held[...] + ring[i, j]
            if j < 5:
                ring_send(i, j + 2)

    def f_at(half, first, second, plane, count):
        return accf.at[pl.ds(2 + 4 * block_at(1 - half, first, second) + 2 * half + plane, count)]

    far_copies, near_copies = {}, {}

    def far_send(h, d):
        for i, st in enumerate(steps):
            far_copies[h, d, i] = send(
                f_at(h, 2, d, i, 1), far_1.at[h, i, pl.ds(d, 1)], axes[1 - h][0], st
            )

    def far_take(h, d):
        for i, st in enumerate(steps):
            far_copies[h, d, i].wait_recv()
            held = f_at(h, st, d, i, 1)
            held[...] = held[...] + far_1[h, i, pl.ds(d, 1)]
            near_copies[h, d, i] = send(
                f_at(h, st, d, 0, 2), near_1.at[h, i, d], axes[1 - h][0], st
            )

    def near_take(h, d):
        for i in range(2):
            near_copies[h, d, i].wait_recv()
        held = f_at(h, 0, d, 0, 2)
        held[...] = held[...] + near_1[h, 0, d] + near_1[h, 1, d]

    order = (2, 1, 3, 0)
    for d in order:
        for h in range(2):
            far_send(h, d)

    @pl.loop(0, 2)
    def _(k):
        backward([u_start(1 - 2 * k, 1), u_start(1 - 2 * k, -1)])

    for h in range(2):
        far_take(h, 2)

    @pl.loop(0, 3)
    def _(k):
        t = k + lax.div(k, 2)
        backward([u_start(2, t), u_start(t, 2)])

    backward([u_start(2, 2)])
    u_halo.wait_recv()
    for q in (0, 65):
        spread(accd, q, 32, [jnp.dot(wd[...], columns(uv[q], masks, -1), preferred_element_type=jnp.float32)])
    for i in range(2):
        ring_send(i, 0)
        ring_send(i, 1)
    for d in (1, 3):
        for h in range(2):
            far_take(h, d)
    weights(0, 2)
    second_far, second_near = {}, {}
    for h in range(2):
        near_take(h, 2)
        for i, st in enumerate(steps):
            second_far[h, i] = send(
                f_at(h, 0, 2, i, 1), far_2.at[h, pl.ds(i, 1)], axes[1 - h][1], st
            )
    for h in range(2):
        far_take(h, 0)
    ring_take(0)
    weights(2, 6)
    weights(6, 9)
    ring_take(1)
    for h in range(2):
        near_take(h, 1)
    weights(9, 12)
    ring_take(2)
    for h in range(2):
        near_take(h, 3)
    for i, st in enumerate(steps):
        for h in range(2):
            second_far[h, i].wait_recv()
            held = f_at(h, 0, st, i, 1)
            held[...] = held[...] + far_2[h, pl.ds(i, 1)]
            second_near[h, i] = send(f_at(h, 0, st, 0, 2), near_2.at[h, i], axes[1 - h][1], st)
    weights(12, 16)
    w_copy = send(accw, other_w, "c", 0)
    ring_take(3)
    for h in range(2):
        near_take(h, 0)
    ring_take(4)
    w_copy.wait_recv()
    out_w[...] = (other_w[...] + accw[...]) / jnp.sqrt(jnp.float32(128 * 256))
    ring_take(5)
    for h in range(2):
        for i in range(2):
            second_near[h, i].wait_recv()
        total = f_at(h, 0, 0, 0, 2)[...] + near_2[h, 0] + near_2[h, 1]
        out_r[2 * h : 2 * h + 2] = total.astype(jnp.bfloat16)
    ring_take(6)
    out_v[...] = accd[pl.ds(2 + 8 * z, 8)].astype(jnp.bfloat16)
    for copy in copies:
        copy.wait_send()


def settle_kernel(r, v, w, out_r, out_v, out_w):
    out_r[...] = r[...]
    out_v[...] = v[...]
    for a in range(3):
        for t in range(9):
            out_w[9 * a + t] = w[32 * t : 32 * t + 32, 64 * (2 - a) : 64 * (3 - a)]


def settled(responses, voxel_grad, weights):
    whole = pl.BlockSpec(memory_space=pltpu.VMEM)
    return pl.pallas_call(
        settle_kernel,
        out_shape=(
            jax.ShapeDtypeStruct(responses.shape, responses.dtype),
            jax.ShapeDtypeStruct(voxel_grad.shape, voxel_grad.dtype),
            jax.ShapeDtypeStruct((27, 32, 64), jnp.float32),
        ),
        in_specs=[whole] * 3,
        out_specs=[whole] * 3,
    )(responses, voxel_grad, weights)


def local(voxels, filters, upstream):
    f32, bf16 = jnp.float32, jnp.bfloat16
    sums = pl.pallas_call(
        full_kernel,
        out_shape=(
            jax.ShapeDtypeStruct((4, 64, 256), bf16),
            jax.ShapeDtypeStruct((8, 32, 256), bf16),
            jax.ShapeDtypeStruct((288, 192), f32),
        ),
        in_specs=[pl.BlockSpec(memory_space=pltpu.VMEM)] * 3,
        out_specs=[pl.BlockSpec(memory_space=pltpu.VMEM)] * 3,
        scratch_shapes=[
            pltpu.VMEM((66, 32, 256), bf16),
            pltpu.VMEM((66, 64, 256), bf16),
            pltpu.VMEM((192, 288), bf16),
            pltpu.VMEM((96, 576), bf16),
            pltpu.VMEM((68, 64, 256), f32),
            pltpu.VMEM((68, 32, 256), f32),
            pltpu.VMEM((288, 192), f32),
            pltpu.VMEM((2, 2, 4, 64, 256), f32),
            pltpu.VMEM((2, 2, 4, 2, 64, 256), f32),
            pltpu.VMEM((2, 2, 64, 256), f32),
            pltpu.VMEM((2, 2, 2, 64, 256), f32),
            pltpu.VMEM((2, 7, 4, 32, 256), f32),
            pltpu.VMEM((288, 192), f32),
            pltpu.SemaphoreType.DMA((COPIES,)),
            pltpu.SemaphoreType.DMA((COPIES,)),
        ],
        compiler_params=pltpu.CompilerParams(
            collective_id=0, has_side_effects=True, vmem_limit_bytes=60 * 2**20
        ),
    )(voxels, filters, upstream)
    return settled(*sums)


def solution(mesh):
    return jax.shard_map(
        local,
        mesh=mesh,
        in_specs=(
            P(("space", "filt"), "chan", None),
            P(None, "chan", "filt"),
            P(("space", "chan"), "filt", None),
        ),
        out_specs=(
            P(("space", "chan"), "filt", None),
            P(("space", "filt"), "chan", None),
            P(None, "chan", "filt"),
        ),
        check_vma=False,
    )
```

```python
import jax
import jax.numpy as jnp
from jax import lax
from jax.experimental import pallas as pl
from jax.experimental.pallas import tpu as pltpu
from jax.sharding import PartitionSpec as P

OFFSETS = [(dy, dz) for dy in (-1, 0, 1) for dz in (-1, 0, 1)]
GROUP = 4
COPIES = 145


def tap_masks():
    lane = lax.broadcasted_iota(jnp.int32, (1, 256), 1)
    z = lane & 15
    y = lane >> 4
    out = []
    for dy, dz in OFFSETS:
        ok = (y + dy >= 0) & (y + dy < 16) & (z + dz >= 0) & (z + dz < 16)
        out.append(jnp.where(ok, 1.0, 0.0).astype(jnp.float32))
    return out


def columns(x, masks, sign):
    parts = []
    for i in range(9):
        dy, dz = OFFSETS[i]
        off = sign * (dy * 16 + dz)
        if off == 0:
            parts.append(x)
            continue
        mask = masks[i if sign > 0 else 8 - i]
        parts.append(pltpu.roll(x, (-off) % 256, 1) * mask.astype(x.dtype))
    return jnp.concatenate(parts, axis=0)


def spread(acc, base, width, ys):
    n = len(ys)
    for i in range(n + 2):
        total = None
        for j in range(max(0, i - 2), min(n, i + 1)):
            part = ys[j][width * (i - j) : width * (i - j + 1), :]
            total = part if total is None else total + part
        acc[base + i] = acc[base + i] + total


def full_kernel(
    vox, fl, up, out_r, out_v, out_w,
    xv, uv, wf, wd, accf, accd, accw, far_1, near_1, far_2, near_2, ring, other_w,
    send_sems, recv_sems,
):
    chan = lax.axis_index("chan")
    z = lax.axis_index("filt")
    core = lax.axis_index("space")
    x = lax.rem(chan, 4)
    y = lax.div(chan, 4)

    def target(axis, step):
        if axis == "z":
            return {"filt": lax.rem(z + step + 8, 8)}
        if axis == "x":
            return {"chan": 4 * y + lax.rem(x + step + 4, 4)}
        if axis == "y":
            return {"chan": 4 * lax.rem(y + step + 4, 4) + x}
        return {"space": 1 - core}

    barrier = pltpu.get_barrier_semaphore()
    for axis, step in (("z", 1), ("z", -1), ("x", 1), ("x", -1), ("y", 1), ("y", -1), ("c", 0)):
        pl.semaphore_signal(
            barrier, inc=1, device_id=target(axis, step), device_id_type=pl.DeviceIdType.MESH
        )
    pl.semaphore_wait(barrier, 7)

    copies = []

    def send(source, dest, axis, step):
        k = len(copies)
        copy = pltpu.make_async_remote_copy(
            src_ref=source,
            dst_ref=dest,
            send_sem=send_sems.at[k],
            recv_sem=recv_sems.at[k],
            device_id=target(axis, step),
            device_id_type=pl.DeviceIdType.MESH,
        )
        copy.start()
        copies.append(copy)
        return copy

    steps = (1, -1)
    axes = (("x", "y"), ("y", "x"))
    place = {"x": x, "y": y}

    def block_at(half, first, second):
        a = lax.rem(place[axes[half][0]] + first + 4, 4)
        b = lax.rem(place[axes[half][1]] + second + 4, 4)
        return (4 * b + a) if half == 0 else (4 * a + b)

    def u_at(half, first, second, plane, count):
        return uv.at[pl.ds(1 + 4 * block_at(half, first, second) + 2 * half + plane, count)]

    def v_at(distance, plane, count):
        return xv.at[pl.ds(1 + 8 * lax.rem(z + distance + 8, 8) + plane, count)]

    first_sent, second_sent = {}, {}
    for turn in range(2):
        for h in range(2):
            for i, st in enumerate(steps):
                n = (i + turn) % 2
                first_sent[h, i, n] = send(
                    up.at[pl.ds(2 * h + n, 1)], u_at(h, 0, 0, n, 1), axes[h][0], st
                )
    z_sent = {}
    for n in range(4):
        for i, st in enumerate(steps):
            part = n if i == 0 else 3 - n
            z_sent[1, i, n] = send(vox.at[pl.ds(2 * part, 2)], v_at(0, 2 * part, 2), "z", st)
    for turn in range(2):
        for h in range(2):
            for i, st in enumerate(steps):
                n = (i + turn) % 2
                second_sent[h, 0, i, n] = send(
                    up.at[pl.ds(2 * h + n, 1)], u_at(h, 0, 0, n, 1), axes[h][1], st
                )

    xv[pl.ds(1 + 8 * z, 8)] = vox[...]
    uv[pl.ds(1 + 4 * chan, 4)] = up[...]
    xv[65 * core] = jnp.zeros((32, 256), jnp.bfloat16)
    uv[65 * core] = jnp.zeros((64, 256), jnp.bfloat16)
    for a in range(3):
        w = fl[9 * a : 9 * a + 9].reshape(288, 64)
        wf[64 * (2 - a) : 64 * (3 - a), :] = w.astype(jnp.float32).T.astype(jnp.bfloat16)
        for t in range(9):
            wd[32 * a : 32 * a + 32, 64 * t : 64 * t + 64] = fl[9 * a + t]
    accf[...] = jnp.zeros_like(accf)
    accd[...] = jnp.zeros_like(accd)
    accw[...] = jnp.zeros_like(accw)
    masks = tap_masks()

    def z_hop(hop, pieces):
        for n in pieces:
            for i, st in enumerate(steps):
                if hop == 4 and n > 1:
                    continue
                z_sent[hop, i, n].wait_recv()
                if hop == 4 or (hop == 3 and n > 1):
                    continue
                piece = v_at(-st * hop, 2 * (n if i == 0 else 3 - n), 2)
                z_sent[hop + 1, i, n] = send(piece, piece, "z", st)

    def pass_second(h, e):
        for turn in range(2):
            for i, st in enumerate(steps):
                n = (i + turn) % 2
                part = u_at(h, e, 0, n, 1)
                second_sent[h, e, i, n] = send(part, part, axes[h][1], st)

    last = []

    def pass_on(h, e):
        for i, st in enumerate(steps):
            second_sent[h, e, i, i].wait_recv()
            part = u_at(h, e, -st, i, 1)
            last.append(send(part, part, axes[h][1], st))

    def rest_of(h, e):
        for i in range(2):
            second_sent[h, e, i, 1 - i].wait_recv()

    def forward(p0):
        ys = [
            jnp.dot(wf[...], columns(xv[p0 + j], masks, 1), preferred_element_type=jnp.float32)
            for j in range(8)
        ]
        spread(accf, p0, 64, ys)

    def backward(starts):
        found = [
            [
                jnp.dot(
                    wd[...], columns(uv[p0 + j], masks, -1), preferred_element_type=jnp.float32
                )
                for j in range(4)
            ]
            for p0 in starts
        ]
        for p0, ys in zip(starts, found):
            spread(accd, p0, 32, ys)

    def forward_at(hop):
        @pl.loop(0, 2)
        def _(k):
            forward(1 + 8 * lax.rem(z + hop * (1 - 2 * k) + 8, 8))

    def u_start(dx, dy):
        return 1 + 4 * (4 * lax.rem(y + dy + 4, 4) + lax.rem(x + dx + 4, 4))

    def weights(low, high):
        @pl.loop(low, high)
        def _(b):
            cols = [columns(xv[b * GROUP + j + 1], masks, 1) for j in range(GROUP)]
            around = [uv[pl.ds(b * GROUP + j, 3)].reshape(192, 256) for j in range(GROUP)]
            accw[...] = accw[...] + lax.dot_general(
                jnp.concatenate(cols, axis=1),
                jnp.concatenate(around, axis=1),
                (((1,), (1,)), ((), ())),
                preferred_element_type=jnp.float32,
            )

    far_sent = [[], []]
    for h in range(2):
        for i, st in enumerate(steps):
            first_sent[h, i, i].wait_recv()
            part = u_at(h, -st, 0, i, 1)
            far_sent[h].append(send(part, part, axes[h][0], st))
    for h in range(2):
        for i in range(2):
            first_sent[h, i, 1 - i].wait_recv()
    for h in range(2):
        pass_second(h, -1)
        pass_second(h, 1)
    z_hop(1, (0, 1))
    for h in range(2):
        pass_on(h, 0)
    z_hop(1, (2, 3))
    forward(1 + 8 * z)
    for h in range(2):
        for copy in far_sent[h]:
            copy.wait_recv()
        pass_second(h, 2)
    z_hop(2, (0, 1))
    forward(1 + 8 * lax.rem(z + 1, 8))
    z_hop(2, (2, 3))
    for h in range(2):
        pass_on(h, -1)
    forward(1 + 8 * lax.rem(z + 7, 8))
    z_hop(3, (0, 1))
    for h in range(2):
        pass_on(h, 1)
    forward(1 + 8 * lax.rem(z + 2, 8))
    z_hop(3, (2, 3))
    for h in range(2):
        pass_on(h, 2)
    forward(1 + 8 * lax.rem(z + 6, 8))
    forward_at(3)
    for h in range(2):
        rest_of(h, 0)
    backward([u_start(0, 0)])

    @pl.loop(0, 2)
    def _(k):
        backward([u_start(1 - 2 * k, 0), u_start(0, 1 - 2 * k)])

    for h in range(2):
        rest_of(h, -1)
        rest_of(h, 1)

    @pl.loop(0, 2)
    def _(k):
        backward([u_start(1 - 2 * k, 1), u_start(1 - 2 * k, -1)])

    z_hop(4, (0, 1))
    inner, outer = 64 - 63 * core, 65 * core
    x_halo = send(xv.at[inner], xv.at[outer], "c", 0)
    forward(1 + 8 * lax.rem(z + 4, 8))
    for h in range(2):
        rest_of(h, 2)
    for copy in last:
        copy.wait_recv()
    u_halo = send(uv.at[inner], uv.at[outer], "c", 0)
    x_halo.wait_recv()
    for q in (0, 65):
        spread(accf, q, 64, [jnp.dot(wf[...], columns(xv[q], masks, 1), preferred_element_type=jnp.float32)])

    def d_at(distance, part):
        return accd.at[pl.ds(2 + 8 * lax.rem(z + distance + 8, 8) + 4 * part, 4)]

    ring_sent = [[], []]

    def ring_send(i, j):
        part = (i + j) % 2
        ring_sent[i].append(
            send(d_at(steps[i] * (4 - (j + 1) // 2), part), ring.at[i, j], "z", steps[i])
        )

    def ring_take(j):
        for i in range(2):
            ring_sent[i][j].wait_recv()
            held = d_at(steps[i] * (3 - (j + 1) // 2), (i + j) % 2)
            held[...] = held[...] + ring[i, j]
            if j < 5:
                ring_send(i, j + 2)

    def f_at(half, first, second, plane, count):
        return accf.at[pl.ds(2 + 4 * block_at(1 - half, first, second) + 2 * half + plane, count)]

    far_copies, near_copies = {}, {}

    def far_send(h, d):
        for i, st in enumerate(steps):
            far_copies[h, d, i] = send(
                f_at(h, 2, d, i, 1), far_1.at[h, i, pl.ds(d, 1)], axes[1 - h][0], st
            )

    def far_take(h, d):
        for i, st in enumerate(steps):
            far_copies[h, d, i].wait_recv()
            held = f_at(h, st, d, i, 1)
            held[...] = held[...] + far_1[h, i, pl.ds(d, 1)]
            near_copies[h, d, i] = send(
                f_at(h, st, d, 0, 2), near_1.at[h, i, d], axes[1 - h][0], st
            )

    def near_take(h, d):
        for i in range(2):
            near_copies[h, d, i].wait_recv()
        held = f_at(h, 0, d, 0, 2)
        held[...] = held[...] + near_1[h, 0, d] + near_1[h, 1, d]

    order = (2, 1, 3, 0)
    for d in order:
        for h in range(2):
            far_send(h, d)

    for h in range(2):
        far_take(h, 2)

    @pl.loop(0, 3)
    def _(k):
        t = k + lax.div(k, 2)
        backward([u_start(2, t), u_start(t, 2)])

    backward([u_start(2, 2)])
    u_halo.wait_recv()
    for q in (0, 65):
        spread(accd, q, 32, [jnp.dot(wd[...], columns(uv[q], masks, -1), preferred_element_type=jnp.float32)])
    for i in range(2):
        ring_send(i, 0)
        ring_send(i, 1)
    for d in (1, 3):
        for h in range(2):
            far_take(h, d)
    weights(0, 2)
    second_far, second_near = {}, {}
    for h in range(2):
        near_take(h, 2)
        for i, st in enumerate(steps):
            second_far[h, i] = send(
                f_at(h, 0, 2, i, 1), far_2.at[h, pl.ds(i, 1)], axes[1 - h][1], st
            )
    for h in range(2):
        far_take(h, 0)
    ring_take(0)
    weights(2, 6)
    weights(6, 9)
    ring_take(1)
    for h in range(2):
        near_take(h, 1)
    weights(9, 12)
    ring_take(2)
    for h in range(2):
        near_take(h, 3)
    for i, st in enumerate(steps):
        for h in range(2):
            second_far[h, i].wait_recv()
            held = f_at(h, 0, st, i, 1)
            held[...] = held[...] + far_2[h, pl.ds(i, 1)]
            second_near[h, i] = send(f_at(h, 0, st, 0, 2), near_2.at[h, i], axes[1 - h][1], st)
    weights(12, 16)
    w_copy = send(accw, other_w, "c", 0)
    ring_take(3)
    for h in range(2):
        near_take(h, 0)
    ring_take(4)
    w_copy.wait_recv()
    out_w[...] = (other_w[...] + accw[...]) / jnp.sqrt(jnp.float32(128 * 256))
    ring_take(5)
    for h in range(2):
        for i in range(2):
            second_near[h, i].wait_recv()
        total = f_at(h, 0, 0, 0, 2)[...] + near_2[h, 0] + near_2[h, 1]
        out_r[2 * h : 2 * h + 2] = total.astype(jnp.bfloat16)
    ring_take(6)
    out_v[...] = accd[pl.ds(2 + 8 * z, 8)].astype(jnp.bfloat16)
    for copy in copies:
        copy.wait_send()


def settle_kernel(r, v, w, out_r, out_v, out_w):
    out_r[...] = r[...]
    out_v[...] = v[...]
    for a in range(3):
        for t in range(9):
            out_w[9 * a + t] = w[32 * t : 32 * t + 32, 64 * (2 - a) : 64 * (3 - a)]


def settled(responses, voxel_grad, weights):
    whole = pl.BlockSpec(memory_space=pltpu.VMEM)
    return pl.pallas_call(
        settle_kernel,
        out_shape=(
            jax.ShapeDtypeStruct(responses.shape, responses.dtype),
            jax.ShapeDtypeStruct(voxel_grad.shape, voxel_grad.dtype),
            jax.ShapeDtypeStruct((27, 32, 64), jnp.float32),
        ),
        in_specs=[whole] * 3,
        out_specs=[whole] * 3,
    )(responses, voxel_grad, weights)


def local(voxels, filters, upstream):
    f32, bf16 = jnp.float32, jnp.bfloat16
    sums = pl.pallas_call(
        full_kernel,
        out_shape=(
            jax.ShapeDtypeStruct((4, 64, 256), bf16),
            jax.ShapeDtypeStruct((8, 32, 256), bf16),
            jax.ShapeDtypeStruct((288, 192), f32),
        ),
        in_specs=[pl.BlockSpec(memory_space=pltpu.VMEM)] * 3,
        out_specs=[pl.BlockSpec(memory_space=pltpu.VMEM)] * 3,
        scratch_shapes=[
            pltpu.VMEM((66, 32, 256), bf16),
            pltpu.VMEM((66, 64, 256), bf16),
            pltpu.VMEM((192, 288), bf16),
            pltpu.VMEM((96, 576), bf16),
            pltpu.VMEM((68, 64, 256), f32),
            pltpu.VMEM((68, 32, 256), f32),
            pltpu.VMEM((288, 192), f32),
            pltpu.VMEM((2, 2, 4, 64, 256), f32),
            pltpu.VMEM((2, 2, 4, 2, 64, 256), f32),
            pltpu.VMEM((2, 2, 64, 256), f32),
            pltpu.VMEM((2, 2, 2, 64, 256), f32),
            pltpu.VMEM((2, 7, 4, 32, 256), f32),
            pltpu.VMEM((288, 192), f32),
            pltpu.SemaphoreType.DMA((COPIES,)),
            pltpu.SemaphoreType.DMA((COPIES,)),
        ],
        compiler_params=pltpu.CompilerParams(
            collective_id=0, has_side_effects=True, vmem_limit_bytes=60 * 2**20
        ),
    )(voxels, filters, upstream)
    return settled(*sums)


def solution(mesh):
    return jax.shard_map(
        local,
        mesh=mesh,
        in_specs=(
            P(("space", "filt"), "chan", None),
            P(None, "chan", "filt"),
            P(("space", "chan"), "filt", None),
        ),
        out_specs=(
            P(("space", "chan"), "filt", None),
            P(("space", "filt"), "chan", None),
            P(None, "chan", "filt"),
        ),
        check_vma=False,
    )
```
